32 devices in a mesh: dp: 8 (over y, x, core), mp: 4 (over z).
Axes of the slice: x: 2, y: 2, z: 4, core: 2. Of those that a mesh axis runs over, the one named last changes fastest.
Arguments:
- pre: bfloat16 [1024, 12288], P('dp', 'mp'), may hold values from -32 to 32
- weight: float32 [6144, 12288], P('dp', 'mp'), may hold values from -0.0546875 to 0.0546875
- target: bfloat16 [6144, 1024], P('dp'), may hold values from -100 to 100
Outputs:
- update: float32 [6144, 12288], P('dp', 'mp')
The draws below stay inside these ranges and needn't reach their ends.
All inputs are finite; a program needn't handle non-finite values.
Results may differ from the reference program's by a relative error of at most 0.0003.
The reference program's roundings to bfloat16 on the way count: a program that leaves them out, or rounds other values in their place, can miss the bound.
Values may be sent and summed in bfloat16 or wider, within the bound.
A program may use at most 64 MiB of HBM per device.

```python
import jax
import jax.numpy as jnp

D = 6144
FF = 12288
TOKENS = 1024


def draw_pre(key, part):
    first, second = jax.random.split(key, 2)
    ramp = jnp.arange(FF, dtype=jnp.float32) / max(FF - 1, 1)
    spread = 10.0 ** jax.random.uniform(second, (FF,), jnp.float32)
    scale = 0.25 * 3.0 ** ramp * spread
    base = jax.random.truncated_normal(first, -4.0, 4.0, (TOKENS, FF), jnp.float32)
    values = scale * base
    return values.astype(jnp.bfloat16)


def draw_target(key, part):
    first, second = jax.random.split(key, 2)
    ramp = jnp.arange(D, dtype=jnp.float32) / max(D - 1, 1)
    spread = 10.0 ** jax.random.uniform(second, (D,), jnp.float32)
    scale = 0.5 * 3.0 ** ramp * spread
    base = jax.random.truncated_normal(first, -4.0, 4.0, (D, TOKENS), jnp.float32)
    values = scale[:, None] * base
    return values.astype(jnp.bfloat16)


def block_levels(own_key, dims, shards, least, top_value):
    def one(axis_at, blocks):
        steps = jax.random.uniform(jax.random.fold_in(jax.random.fold_in(own_key, 6), axis_at), (blocks,), jnp.float32, least / len(shards), top_value / len(shards))
        return jnp.repeat(jnp.exp(steps), dims[axis_at] // blocks).reshape((-1,) + (1,) * (len(dims) - axis_at - 1))

    gain = one(*shards[0])
    for cut in shards[1:]:
        gain = gain * one(*cut)
    return gain


def normal_values(rng, shape, scale, limit, shards=(), kind=jnp.bfloat16):
    drawn = scale * jax.random.normal(rng, shape, jnp.float32)
    if shards:
        drawn = drawn * block_levels(rng, shape, shards, -0.22, 0.18)
    return jnp.clip(drawn, -limit, limit).astype(kind)


def setup_inputs(seed: int = 0) -> dict:
    seeds = jax.random.split(jax.random.key(seed), 4)
    return {
        "pre": draw_pre(jax.random.fold_in(seeds[3], 71), 0),
        "weight": normal_values(seeds[1], (D, FF), FF ** -0.5, 0.0546875, ((0, 8), (1, 4)), jnp.float32),
        "target": draw_target(jax.random.fold_in(seeds[3], 71), 0),
    }


radius = 0.005
epsilon = 1e-06

def residual_of(matrix, hidden, target):
    out = jnp.dot(matrix, hidden.T, preferred_element_type=jnp.float32)
    return (out - target.astype(jnp.float32)).astype(jnp.bfloat16)

def reference(pre, weight, target):
    hidden = jax.nn.gelu(pre.astype(jnp.float32), approximate=False).astype(jnp.bfloat16)
    resid = residual_of(weight.astype(jnp.bfloat16), hidden, target)
    ascent = jnp.dot(resid, hidden, preferred_element_type=jnp.float32)
    ascent_ms = jnp.mean(ascent * ascent)
    perturbed = (weight + radius * jnp.tanh(ascent / jnp.sqrt(ascent_ms + epsilon))).astype(jnp.bfloat16)
    resid_two = residual_of(perturbed, hidden, target)
    descent = jnp.dot(resid_two, hidden, preferred_element_type=jnp.float32)
    descent_ms = jnp.mean(descent * descent)
    return descent / jnp.sqrt(descent_ms + epsilon)
```

```python
import functools

import jax
import jax.numpy as jnp
from jax import lax
from jax.experimental import pallas as pl
from jax.experimental.pallas import tpu as pltpu
from jax.sharding import PartitionSpec as P

radius = 0.005
epsilon = 1e-06
LAG = 1
MESH = pl.DeviceIdType.MESH


def on_device_plain(pre, weight, target):
    hidden = jax.nn.gelu(pre.astype(jnp.float32), approximate=False).astype(jnp.bfloat16)
    everyone = lax.all_gather(hidden, "dp", axis=0, tiled=True)
    entries = weight.shape[0] * weight.shape[1] * lax.axis_size("dp") * lax.axis_size("mp")

    def residual_of(matrix):
        partial_out = lax.dot_general(
            matrix, everyone, (((1,), (1,)), ((), ())), preferred_element_type=jnp.float32
        )
        summed = lax.psum(partial_out, "mp")
        return (summed - target.astype(jnp.float32)).astype(jnp.bfloat16)

    resid = residual_of(weight.astype(jnp.bfloat16))
    ascent = jnp.dot(resid, everyone, preferred_element_type=jnp.float32)
    ascent_ms = lax.psum(jnp.sum(ascent * ascent), ("dp", "mp")) / entries
    perturbed = (weight + radius * jnp.tanh(ascent / jnp.sqrt(ascent_ms + epsilon))).astype(
        jnp.bfloat16
    )
    resid_two = residual_of(perturbed)
    descent = jnp.dot(resid_two, everyone, preferred_element_type=jnp.float32)
    descent_ms = lax.psum(jnp.sum(descent * descent), ("dp", "mp")) / entries
    return descent / jnp.sqrt(descent_ms + epsilon)


def kernel(
    N, M, entries, C,
    hid_hbm, w_hbm, t_hbm, des_hbm, tot_ref,
    w, wl, h, a, tg, r1, r2, own1, own2, rcv1, rcv2, pbuf, ssq, sm, sd, dsum,
    ld, ags, agr, cs, cr, ss, sr, od,
):
    rows, ff = w.shape
    tokens = tg.shape[1]
    blk = tokens // N
    half = rows // 2
    dp = lax.axis_index("dp")
    z = lax.axis_index("mp")
    b0 = lax.rem(dp, 2)
    b1 = lax.rem(dp // 2, 2)
    b2 = dp // 4
    ds_ = 1 - 2 * b0
    dx = 2 * (1 - 2 * b1)
    dy = 4 * (1 - 2 * b2)
    sib = dp + ds_
    p = dp + (1 - b0) * dx + b0 * dy
    q = dp + b0 * dx + (1 - b0) * dy
    diag = dp + dx + dy
    sibp = q + ds_
    sibq = p + ds_
    sibd = diag + ds_

    def load(i, src, dst):
        return pltpu.make_async_copy(src, dst, ld.at[i])

    def tok(b, lo=0, n=blk):
        return pl.ds(pl.multiple_of(b * blk + lo, 16), n)

    load_h = load(0, hid_hbm, h.at[tok(dp), :])
    load_w = load(1, w_hbm, w)
    load_t = load(2, t_hbm, tg)
    load_h.start()
    load_w.start()
    load_t.start()

    barrier = pltpu.get_barrier_semaphore()
    for k in range(1, N):
        pl.semaphore_signal(barrier, inc=1, device_id=(lax.rem(dp + k, N), z), device_id_type=MESH)
    for k in range(1, M):
        pl.semaphore_signal(barrier, inc=1, device_id=(dp, lax.rem(z + k, M)), device_id_type=MESH)
    pl.semaphore_wait(barrier, N + M - 2)

    def gather(i, block, to, lo=0, n=blk):
        return pltpu.make_async_remote_copy(
            src_ref=h.at[tok(block, lo, n), :], dst_ref=h.at[tok(block, lo, n), :],
            send_sem=ags.at[i], recv_sem=agr.at[i],
            device_id=(to, z), device_id_type=MESH,
        )

    hb = blk // 2
    S, PP, Q, SP, SQ, RPQ, RQP, SD = range(8)
    sends = {
        S: gather(S, dp, sib), PP: gather(PP, dp, p), Q: gather(Q, dp, q),
        SP: gather(SP, p, sib), SQ: gather(SQ, q, sib),
        RPQ: gather(RPQ, p, q, 0, hb), RQP: gather(RQP, q, p, hb, hb),
        SD: gather(SD, diag, sib),
    }
    recvs = {
        S: gather(S, sib, sib), PP: gather(PP, p, p), Q: gather(Q, q, q),
        SP: gather(SP, sibp, sib), SQ: gather(SQ, sibq, sib),
        RPQ: gather(RPQ, diag, q, 0, hb), RQP: gather(RQP, diag, p, hb, hb),
        SD: gather(SD, sibd, sib),
    }
    load_h.wait()
    sends[PP].start()
    sends[S].start()
    load_w.wait()

    def cast(i, _):
        rs = pl.ds(pl.multiple_of(i * 64, 64), 64)
        wl[rs, :] = w[rs, :].astype(jnp.bfloat16)
        return 0

    lax.fori_loop(0, rows // 64, cast, 0)
    load_t.wait()

    order = [dp, sib, p, sibp, q, sibq, diag, sibd]

    def block_of(c):
        out = order[0] * 0
        for k in range(N):
            out = out + order[k] * (1 - jnp.minimum(jnp.abs(c - k), 1))
        return out

    UP, DOWN, RUP, RDOWN = range(4)

    def move(kind, c, src, dst, to):
        return pltpu.make_async_remote_copy(
            src_ref=src, dst_ref=dst, send_sem=cs.at[kind, c], recv_sem=cr.at[kind, c],
            device_id=(dp, to), device_id_type=MESH,
        )

    zu = lax.rem(z + 1, M)
    zd = lax.rem(z + M - 1, M)

    def chain(produce, own_at, rcv_at, res_at, tgt_of, on_up, on_down):
        def step(s, _):
            @pl.when(s < C)
            def _():
                produce(s)

            def reduce_one(kind, rkind, which, lag, is_head, is_tail, to, back):
                c = s - lag

                @pl.when((c >= 0) & (c < C))
                def _():
                    own = own_at(c, which)

                    @pl.when(jnp.logical_not(is_head))
                    def _():
                        move(kind, c, own, rcv_at(c, which), to).wait_recv()

                    @pl.when(jnp.logical_not(is_head | is_tail))
                    def _():
                        own[...] = own[...] + rcv_at(c, which)[...]

                    @pl.when(jnp.logical_not(is_tail))
                    def _():
                        move(kind, c, own, rcv_at(c, which), to).start()

                    @pl.when(is_tail)
                    def _():
                        total = own[...] + rcv_at(c, which)[...]
                        res_at(c, which)[...] = (
                            total - tgt_of(c, which)[...].astype(jnp.float32)
                        ).astype(jnp.bfloat16)
                        move(rkind, c, res_at(c, which), res_at(c, which), back).start()

            def back_one(rkind, which, lag, is_owner, is_last, to, done):
                c = s - lag

                @pl.when((c >= 0) & (c < C))
                def _():
                    @pl.when(jnp.logical_not(is_owner))
                    def _():
                        m = move(rkind, c, res_at(c, which), res_at(c, which), to)
                        m.wait_recv()

                        @pl.when(jnp.logical_not(is_last))
                        def _():
                            m.start()

                    if done is not None:
                        done(c)

            first, last = z == 0, z == M - 1
            reduce_one(UP, RUP, 0, LAG * z, first, last, zu, zd)
            reduce_one(DOWN, RDOWN, 1, LAG * (M - 1 - z), last, first, zd, zu)
            back_one(RUP, 0, LAG * (2 * (M - 1) - z), last, first, zd, on_up)
            back_one(RDOWN, 1, LAG * (M - 1 + z), first, last, zu, on_down)
            return 0

        lax.fori_loop(0, C + 2 * LAG * (M - 1), step, 0)

        def drain(c, _):
            @pl.when(z < M - 1)
            def _():
                move(UP, c, own_at(c, 0), rcv_at(c, 0), zu).wait_send()
                move(RDOWN, c, res_at(c, 1), res_at(c, 1), zu).wait_send()

            @pl.when(z > 0)
            def _():
                move(DOWN, c, own_at(c, 1), rcv_at(c, 1), zd).wait_send()
                move(RUP, c, res_at(c, 0), res_at(c, 0), zd).wait_send()

            return 0

        lax.fori_loop(0, C, drain, 0)

    def produce_one(s):
        @pl.when(s == 1)
        def _():
            recvs[S].wait_recv()

        @pl.when(s == 2)
        def _():
            recvs[PP].wait_recv()
            sends[SP].start()
            sends[Q].start()

        @pl.when(s == 3)
        def _():
            recvs[SP].wait_recv()

        @pl.when(s == 4)
        def _():
            recvs[Q].wait_recv()
            sends[RPQ].start()
            sends[RQP].start()
            sends[SQ].start()

        @pl.when(s == 5)
        def _():
            recvs[SQ].wait_recv()

        @pl.when(s == 6)
        def _():
            recvs[RPQ].wait_recv()
            recvs[RQP].wait_recv()
            sends[SD].start()

        @pl.when(s == 7)
        def _():
            recvs[SD].wait_recv()

        hb_ = h[tok(block_of(s)), :]
        own1[s] = lax.dot_general(
            wl[...], hb_, (((1,), (1,)), ((), ())), preferred_element_type=jnp.float32
        )

    def cols(c):
        return pl.ds(pl.multiple_of(block_of(c) * blk, blk), blk)

    def one(ref):
        return lambda c, which: ref.at[c, pl.ds(which * half, half), :]

    def colwise(ref):
        return lambda c, which: ref.at[pl.ds(which * half, half), cols(c)]

    chain(produce_one, one(own1), one(rcv1), colwise(r1), colwise(tg), None, None)
    for i in range(8):
        sends[i].wait_send()

    def total_squares(rnd):
        v = ssq[...]
        part = v[:, 0:128]
        for k in range(1, v.shape[1] // 128):
            part = part + v[:, 128 * k:128 * (k + 1)]

        def small(buf, lane, i, me, to):
            return pltpu.make_async_remote_copy(
                src_ref=buf.at[me], dst_ref=buf.at[me],
                send_sem=ss.at[rnd, lane, i], recv_sem=sr.at[rnd, lane, i],
                device_id=to, device_id_type=MESH,
            )

        mb = sm.at[rnd]
        db = sd.at[rnd]
        mb[z] = part
        up = [(dp, lax.rem(z + k, M)) for k in range(M)]
        dn = [lax.rem(z + M - k, M) for k in range(M)]
        for k in range(1, M):
            small(mb, 0, k, z, up[k]).start()
        for k in range(1, M):
            small(mb, 0, k, dn[k], up[k]).wait_recv()
        for k in range(1, M):
            small(mb, 0, k, z, up[k]).wait_send()
        got = mb[0]
        for k in range(1, M):
            got = got + mb[k]
        db[dp] = got
        upd = [(lax.rem(dp + k, N), z) for k in range(N)]
        dnd = [lax.rem(dp + N - k, N) for k in range(N)]
        for k in range(1, N):
            small(db, 1, k, dp, upd[k]).start()
        for k in range(1, N):
            small(db, 1, k, dnd[k], upd[k]).wait_recv()
        for k in range(1, N):
            small(db, 1, k, dp, upd[k]).wait_send()
        got = db[0]
        for k in range(1, N):
            got = got + db[k]
        return jnp.sum(jnp.sum(got, axis=0, keepdims=True), axis=1, keepdims=True)

    def squares(d):
        return (d * d).reshape(d.shape[0] // 8, 8, d.shape[1]).sum(axis=0)

    wide = ssq.shape[1]
    ssq[...] = jnp.zeros_like(ssq)

    def ascend(i, _):
        cs_ = pl.ds(pl.multiple_of(i * wide, wide), wide)
        d = jnp.dot(r1[...], h[:, cs_], preferred_element_type=jnp.float32)
        a[:, cs_] = d
        ssq[...] += squares(d)
        return 0

    lax.fori_loop(0, ff // wide, ascend, 0)
    scale = 1.0 / jnp.sqrt(total_squares(0) / entries + epsilon)
    ssq[...] = jnp.zeros_like(ssq)

    sub = half // C
    strip = tokens // 4

    def rws(c, which):
        return pl.ds(pl.multiple_of(which * half + c * sub, 16), sub)

    def produce_two(s):
        for which in range(2):
            rs = rws(s, which)
            pbuf[which * sub:(which + 1) * sub, :] = (
                w[rs, :] + radius * jnp.tanh(a[rs, :] * scale)
            ).astype(jnp.bfloat16)

        def part(i, _):
            ts = pl.ds(pl.multiple_of(i * strip, strip), strip)
            d = lax.dot_general(
                pbuf[...], h[ts, :], (((1,), (1,)), ((), ())), preferred_element_type=jnp.float32
            )
            own2[rws(s, 0), ts] = d[:sub]
            own2[rws(s, 1), ts] = d[sub:]
            return 0

        lax.fori_loop(0, tokens // strip, part, 0)

    def out_copy(c, which):
        return pltpu.make_async_copy(a.at[rws(c, which), :], des_hbm.at[rws(c, which), :], od.at[which, c])

    def descend(which):
        def run(c):
            def part(i, _):
                cs_ = pl.ds(pl.multiple_of(i * wide, wide), wide)
                d = jnp.dot(r2[rws(c, which), :], h[:, cs_], preferred_element_type=jnp.float32)
                a[rws(c, which), cs_] = d
                ssq[...] += squares(d)
                return 0

            lax.fori_loop(0, ff // wide, part, 0)
            out_copy(c, which).start()

        return run

    def rowwise(ref):
        return lambda c, which: ref.at[rws(c, which), :]

    chain(produce_two, rowwise(own2), rowwise(rcv2), rowwise(r2), rowwise(tg), descend(0), descend(1))
    tot_ref[...] = jnp.broadcast_to(total_squares(1), tot_ref.shape)

    def drain_out(c, _):
        out_copy(c, 0).wait()
        out_copy(c, 1).wait()
        return 0

    lax.fori_loop(0, C, drain_out, 0)


def on_device(N, M, pre, weight, target):
    hidden = jax.nn.gelu(pre.astype(jnp.float32), approximate=False).astype(jnp.bfloat16)
    rows, ff = weight.shape
    tokens = target.shape[1]
    entries = rows * ff * N * M
    C = N
    f32, bf16 = jnp.float32, jnp.bfloat16
    half = rows // 2
    blk = tokens // N
    any_ = pl.BlockSpec(memory_space=pl.ANY)
    descent, total = pl.pallas_call(
        functools.partial(kernel, N, M, float(entries), C),
        out_shape=(
            jax.ShapeDtypeStruct((rows, ff), f32),
            jax.ShapeDtypeStruct((8, 128), f32),
        ),
        in_specs=[any_, any_, any_],
        out_specs=(any_, pl.BlockSpec(memory_space=pltpu.VMEM)),
        scratch_shapes=[
            pltpu.VMEM((rows, ff), f32),
            pltpu.VMEM((rows, ff), bf16),
            pltpu.VMEM((tokens, ff), bf16),
            pltpu.VMEM((rows, ff), f32),
            pltpu.VMEM((rows, tokens), bf16),
            pltpu.VMEM((rows, tokens), bf16),
            pltpu.VMEM((rows, tokens), bf16),
            pltpu.VMEM((N, rows, blk), f32),
            pltpu.VMEM((rows, tokens), f32),
            pltpu.VMEM((N, rows, blk), f32),
            pltpu.VMEM((rows, tokens), f32),
            pltpu.VMEM((2 * half // C, ff), bf16),
            pltpu.VMEM((8, 512), f32),
            pltpu.VMEM((2, M, 8, 128), f32),
            pltpu.VMEM((2, N, 8, 128), f32),
            pltpu.VMEM((8, 128), f32),
            pltpu.SemaphoreType.DMA((3,)),
            pltpu.SemaphoreType.DMA((8,)),
            pltpu.SemaphoreType.DMA((8,)),
            pltpu.SemaphoreType.DMA((4, C)),
            pltpu.SemaphoreType.DMA((4, C)),
            pltpu.SemaphoreType.DMA((2, 2, max(N, M))),
            pltpu.SemaphoreType.DMA((2, 2, max(N, M))),
            pltpu.SemaphoreType.DMA((2, C)),
        ],
        compiler_params=pltpu.CompilerParams(
            collective_id=0, has_side_effects=True, vmem_limit_bytes=60 << 20
        ),
    )(hidden, weight, target)
    return descent / jnp.sqrt(total[0, 0] / entries + epsilon)


def solution(mesh):
    N, M = mesh.shape["dp"], mesh.shape["mp"]
    body = functools.partial(on_device, N, M) if (N, M) == (8, 4) else on_device_plain
    return jax.shard_map(
        body,
        mesh=mesh,
        in_specs=(P("dp", "mp"), P("dp", "mp"), P("dp", None)),
        out_specs=P("dp", "mp"),
        check_vma=False,
    )
```

```python
import functools

import jax
import jax.numpy as jnp
from jax import lax
from jax.experimental import pallas as pl
from jax.experimental.pallas import tpu as pltpu
from jax.sharding import PartitionSpec as P

radius = 0.005
epsilon = 1e-06
LAG = 1
MESH = pl.DeviceIdType.MESH


def on_device_plain(pre, weight, target):
    hidden = jax.nn.gelu(pre.astype(jnp.float32), approximate=False).astype(jnp.bfloat16)
    everyone = lax.all_gather(hidden, "dp", axis=0, tiled=True)
    entries = weight.shape[0] * weight.shape[1] * lax.axis_size("dp") * lax.axis_size("mp")

    def residual_of(matrix):
        partial_out = lax.dot_general(
            matrix, everyone, (((1,), (1,)), ((), ())), preferred_element_type=jnp.float32
        )
        summed = lax.psum(partial_out, "mp")
        return (summed - target.astype(jnp.float32)).astype(jnp.bfloat16)

    resid = residual_of(weight.astype(jnp.bfloat16))
    ascent = jnp.dot(resid, everyone, preferred_element_type=jnp.float32)
    ascent_ms = lax.psum(jnp.sum(ascent * ascent), ("dp", "mp")) / entries
    perturbed = (weight + radius * jnp.tanh(ascent / jnp.sqrt(ascent_ms + epsilon))).astype(
        jnp.bfloat16
    )
    resid_two = residual_of(perturbed)
    descent = jnp.dot(resid_two, everyone, preferred_element_type=jnp.float32)
    descent_ms = lax.psum(jnp.sum(descent * descent), ("dp", "mp")) / entries
    return descent / jnp.sqrt(descent_ms + epsilon)


def kernel(
    N, M, entries, C,
    hid_hbm, w_hbm, t_hbm, des_hbm, tot_ref,
    w, wl, h, a, tg, r1, own1, rcv1, pbuf, ssq, sm, sd, dsum,
    ld, ags, agr, cs, cr, ss, sr, od,
):
    rows, ff = w.shape
    tokens = tg.shape[1]
    blk = tokens // N
    half = rows // 2
    dp = lax.axis_index("dp")
    z = lax.axis_index("mp")
    b0 = lax.rem(dp, 2)
    b1 = lax.rem(dp // 2, 2)
    b2 = dp // 4
    ds_ = 1 - 2 * b0
    dx = 2 * (1 - 2 * b1)
    dy = 4 * (1 - 2 * b2)
    sib = dp + ds_
    p = dp + (1 - b0) * dx + b0 * dy
    q = dp + b0 * dx + (1 - b0) * dy
    diag = dp + dx + dy
    sibp = q + ds_
    sibq = p + ds_
    sibd = diag + ds_

    def load(i, src, dst):
        return pltpu.make_async_copy(src, dst, ld.at[i])

    def tok(b, lo=0, n=blk):
        return pl.ds(pl.multiple_of(b * blk + lo, 16), n)

    load_h = load(0, hid_hbm, h.at[tok(dp), :])
    load_w = load(1, w_hbm, w)
    load_t = load(2, t_hbm, tg)
    load_h.start()
    load_w.start()
    load_t.start()

    barrier = pltpu.get_barrier_semaphore()
    for k in range(1, N):
        pl.semaphore_signal(barrier, inc=1, device_id=(lax.rem(dp + k, N), z), device_id_type=MESH)
    for k in range(1, M):
        pl.semaphore_signal(barrier, inc=1, device_id=(dp, lax.rem(z + k, M)), device_id_type=MESH)
    pl.semaphore_wait(barrier, N + M - 2)

    def gather(i, block, to, lo=0, n=blk):
        return pltpu.make_async_remote_copy(
            src_ref=h.at[tok(block, lo, n), :], dst_ref=h.at[tok(block, lo, n), :],
            send_sem=ags.at[i], recv_sem=agr.at[i],
            device_id=(to, z), device_id_type=MESH,
        )

    hb = blk // 2
    S, PP, Q, SP, SQ, RPQ, RQP, SD = range(8)
    sends = {
        S: gather(S, dp, sib), PP: gather(PP, dp, p), Q: gather(Q, dp, q),
        SP: gather(SP, p, sib), SQ: gather(SQ, q, sib),
        RPQ: gather(RPQ, p, q, 0, hb), RQP: gather(RQP, q, p, hb, hb),
        SD: gather(SD, diag, sib),
    }
    recvs = {
        S: gather(S, sib, sib), PP: gather(PP, p, p), Q: gather(Q, q, q),
        SP: gather(SP, sibp, sib), SQ: gather(SQ, sibq, sib),
        RPQ: gather(RPQ, diag, q, 0, hb), RQP: gather(RQP, diag, p, hb, hb),
        SD: gather(SD, sibd, sib),
    }
    load_h.wait()
    sends[PP].start()
    sends[S].start()
    load_w.wait()

    def cast(i, _):
        rs = pl.ds(pl.multiple_of(i * 64, 64), 64)
        wl[rs, :] = w[rs, :].astype(jnp.bfloat16)
        return 0

    lax.fori_loop(0, rows // 64, cast, 0)
    load_t.wait()

    order = [dp, sib, p, sibp, q, sibq, diag, sibd]

    def block_of(c):
        out = order[0] * 0
        for k in range(N):
            out = out + order[k] * (1 - jnp.minimum(jnp.abs(c - k), 1))
        return out

    UP, DOWN, RUP, RDOWN = range(4)

    def move(kind, c, src, dst, to):
        return pltpu.make_async_remote_copy(
            src_ref=src, dst_ref=dst, send_sem=cs.at[kind, c], recv_sem=cr.at[kind, c],
            device_id=(dp, to), device_id_type=MESH,
        )

    zu = lax.rem(z + 1, M)
    zd = lax.rem(z + M - 1, M)

    def chain(produce, own_at, rcv_at, res_at, tgt_of, on_up, on_down):
        def step(s, _):
            @pl.when(s < C)
            def _():
                produce(s)

            def reduce_one(kind, rkind, which, lag, is_head, is_tail, to, back):
                c = s - lag

                @pl.when((c >= 0) & (c < C))
                def _():
                    own = own_at(c, which)

                    @pl.when(jnp.logical_not(is_head))
                    def _():
                        move(kind, c, own, rcv_at(c, which), to).wait_recv()

                    @pl.when(jnp.logical_not(is_head | is_tail))
                    def _():
                        own[...] = own[...] + rcv_at(c, which)[...]

                    @pl.when(jnp.logical_not(is_tail))
                    def _():
                        move(kind, c, own, rcv_at(c, which), to).start()

                    @pl.when(is_tail)
                    def _():
                        total = own[...] + rcv_at(c, which)[...]
                        res_at(c, which)[...] = (
                            total - tgt_of(c, which)[...].astype(jnp.float32)
                        ).astype(jnp.bfloat16)
                        move(rkind, c, res_at(c, which), res_at(c, which), back).start()

            def back_one(rkind, which, lag, is_owner, is_last, to, done):
                c = s - lag

                @pl.when((c >= 0) & (c < C))
                def _():
                    @pl.when(jnp.logical_not(is_owner))
                    def _():
                        m = move(rkind, c, res_at(c, which), res_at(c, which), to)
                        m.wait_recv()

                        @pl.when(jnp.logical_not(is_last))
                        def _():
                            m.start()

                    if done is not None:
                        done(c)

            first, last = z == 0, z == M - 1
            reduce_one(UP, RUP, 0, LAG * z, first, last, zu, zd)
            reduce_one(DOWN, RDOWN, 1, LAG * (M - 1 - z), last, first, zd, zu)
            back_one(RUP, 0, LAG * (2 * (M - 1) - z), last, first, zd, on_up)
            back_one(RDOWN, 1, LAG * (M - 1 + z), first, last, zu, on_down)
            return 0

        lax.fori_loop(0, C + 2 * LAG * (M - 1), step, 0)

        def drain(c, _):
            @pl.when(z < M - 1)
            def _():
                move(UP, c, own_at(c, 0), rcv_at(c, 0), zu).wait_send()
                move(RDOWN, c, res_at(c, 1), res_at(c, 1), zu).wait_send()

            @pl.when(z > 0)
            def _():
                move(DOWN, c, own_at(c, 1), rcv_at(c, 1), zd).wait_send()
                move(RUP, c, res_at(c, 0), res_at(c, 0), zd).wait_send()

            return 0

        lax.fori_loop(0, C, drain, 0)

    def produce_one(s):
        @pl.when(s == 1)
        def _():
            recvs[S].wait_recv()

        @pl.when(s == 2)
        def _():
            recvs[PP].wait_recv()
            sends[SP].start()
            sends[Q].start()

        @pl.when(s == 3)
        def _():
            recvs[SP].wait_recv()

        @pl.when(s == 4)
        def _():
            recvs[Q].wait_recv()
            sends[RPQ].start()
            sends[RQP].start()
            sends[SQ].start()

        @pl.when(s == 5)
        def _():
            recvs[SQ].wait_recv()

        @pl.when(s == 6)
        def _():
            recvs[RPQ].wait_recv()
            recvs[RQP].wait_recv()
            sends[SD].start()

        @pl.when(s == 7)
        def _():
            recvs[SD].wait_recv()

        hb_ = h[tok(block_of(s)), :]
        own1[:, cols(s)] = lax.dot_general(
            wl[...], hb_, (((1,), (1,)), ((), ())), preferred_element_type=jnp.float32
        )

    def cols(c):
        return pl.ds(pl.multiple_of(block_of(c) * blk, blk), blk)

    def colwise(ref):
        return lambda c, which: ref.at[pl.ds(which * half, half), cols(c)]

    chain(produce_one, colwise(own1), colwise(rcv1), colwise(r1), colwise(tg), None, None)
    for i in range(8):
        sends[i].wait_send()

    def total_squares(rnd):
        v = ssq[...]
        part = v[:, 0:128]
        for k in range(1, v.shape[1] // 128):
            part = part + v[:, 128 * k:128 * (k + 1)]

        def small(buf, lane, i, me, to):
            return pltpu.make_async_remote_copy(
                src_ref=buf.at[me], dst_ref=buf.at[me],
                send_sem=ss.at[rnd, lane, i], recv_sem=sr.at[rnd, lane, i],
                device_id=to, device_id_type=MESH,
            )

        mb = sm.at[rnd]
        db = sd.at[rnd]
        mb[z] = part
        up = [(dp, lax.rem(z + k, M)) for k in range(M)]
        dn = [lax.rem(z + M - k, M) for k in range(M)]
        for k in range(1, M):
            small(mb, 0, k, z, up[k]).start()
        for k in range(1, M):
            small(mb, 0, k, dn[k], up[k]).wait_recv()
        for k in range(1, M):
            small(mb, 0, k, z, up[k]).wait_send()
        got = mb[0]
        for k in range(1, M):
            got = got + mb[k]
        db[dp] = got
        upd = [(lax.rem(dp + k, N), z) for k in range(N)]
        dnd = [lax.rem(dp + N - k, N) for k in range(N)]
        for k in range(1, N):
            small(db, 1, k, dp, upd[k]).start()
        for k in range(1, N):
            small(db, 1, k, dnd[k], upd[k]).wait_recv()
        for k in range(1, N):
            small(db, 1, k, dp, upd[k]).wait_send()
        got = db[0]
        for k in range(1, N):
            got = got + db[k]
        return jnp.sum(jnp.sum(got, axis=0, keepdims=True), axis=1, keepdims=True)

    def squares(d):
        return (d * d).reshape(d.shape[0] // 8, 8, d.shape[1]).sum(axis=0)

    wide = ssq.shape[1]
    ssq[...] = jnp.zeros_like(ssq)

    def ascend(i, _):
        cs_ = pl.ds(pl.multiple_of(i * wide, wide), wide)
        d = jnp.dot(r1[...], h[:, cs_], preferred_element_type=jnp.float32)
        a[:, cs_] = d
        ssq[...] += squares(d)
        return 0

    lax.fori_loop(0, ff // wide, ascend, 0)
    scale = 1.0 / jnp.sqrt(total_squares(0) / entries + epsilon)
    ssq[...] = jnp.zeros_like(ssq)

    sub = half // C
    strip = tokens // 4

    def rws(c, which):
        return pl.ds(pl.multiple_of(which * half + c * sub, 16), sub)

    def produce_two(s):
        for which in range(2):
            rs = rws(s, which)
            pbuf[which * sub:(which + 1) * sub, :] = (
                w[rs, :] + radius * jnp.tanh(a[rs, :] * scale)
            ).astype(jnp.bfloat16)

        def part(i, _):
            ts = pl.ds(pl.multiple_of(i * strip, strip), strip)
            d = lax.dot_general(
                pbuf[...], h[ts, :], (((1,), (1,)), ((), ())), preferred_element_type=jnp.float32
            )
            own1[rws(s, 0), ts] = d[:sub]
            own1[rws(s, 1), ts] = d[sub:]
            return 0

        lax.fori_loop(0, tokens // strip, part, 0)

    def out_copy(c, which):
        return pltpu.make_async_copy(a.at[rws(c, which), :], des_hbm.at[rws(c, which), :], od.at[which, c])

    def descend(which):
        def run(c):
            def part(i, _):
                cs_ = pl.ds(pl.multiple_of(i * wide, wide), wide)
                d = jnp.dot(r1[rws(c, which), :], h[:, cs_], preferred_element_type=jnp.float32)
                a[rws(c, which), cs_] = d
                ssq[...] += squares(d)
                return 0

            lax.fori_loop(0, ff // wide, part, 0)
            out_copy(c, which).start()

        return run

    def rowwise(ref):
        return lambda c, which: ref.at[rws(c, which), :]

    chain(produce_two, rowwise(own1), rowwise(rcv1), rowwise(r1), rowwise(tg), descend(0), descend(1))
    tot_ref[...] = jnp.broadcast_to(total_squares(1), tot_ref.shape)

    def drain_out(c, _):
        out_copy(c, 0).wait()
        out_copy(c, 1).wait()
        return 0

    lax.fori_loop(0, C, drain_out, 0)


def on_device(N, M, pre, weight, target):
    hidden = jax.nn.gelu(pre.astype(jnp.float32), approximate=False).astype(jnp.bfloat16)
    rows, ff = weight.shape
    tokens = target.shape[1]
    entries = rows * ff * N * M
    C = N
    f32, bf16 = jnp.float32, jnp.bfloat16
    half = rows // 2
    any_ = pl.BlockSpec(memory_space=pl.ANY)
    descent, total = pl.pallas_call(
        functools.partial(kernel, N, M, float(entries), C),
        out_shape=(
            jax.ShapeDtypeStruct((rows, ff), f32),
            jax.ShapeDtypeStruct((8, 128), f32),
        ),
        in_specs=[any_, any_, any_],
        out_specs=(any_, pl.BlockSpec(memory_space=pltpu.VMEM)),
        scratch_shapes=[
            pltpu.VMEM((rows, ff), f32),
            pltpu.VMEM((rows, ff), bf16),
            pltpu.VMEM((tokens, ff), bf16),
            pltpu.VMEM((rows, ff), f32),
            pltpu.VMEM((rows, tokens), bf16),
            pltpu.VMEM((rows, tokens), bf16),
            pltpu.VMEM((rows, tokens), f32),
            pltpu.VMEM((rows, tokens), f32),
            pltpu.VMEM((2 * half // C, ff), bf16),
            pltpu.VMEM((8, 512), f32),
            pltpu.VMEM((2, M, 8, 128), f32),
            pltpu.VMEM((2, N, 8, 128), f32),
            pltpu.VMEM((8, 128), f32),
            pltpu.SemaphoreType.DMA((3,)),
            pltpu.SemaphoreType.DMA((8,)),
            pltpu.SemaphoreType.DMA((8,)),
            pltpu.SemaphoreType.DMA((4, C)),
            pltpu.SemaphoreType.DMA((4, C)),
            pltpu.SemaphoreType.DMA((2, 2, max(N, M))),
            pltpu.SemaphoreType.DMA((2, 2, max(N, M))),
            pltpu.SemaphoreType.DMA((2, C)),
        ],
        compiler_params=pltpu.CompilerParams(
            collective_id=0, has_side_effects=True, vmem_limit_bytes=41 << 20
        ),
    )(hidden, weight, target)
    return descent * (1.0 / jnp.sqrt(total[0, 0] / entries + epsilon))


def solution(mesh):
    N, M = mesh.shape["dp"], mesh.shape["mp"]
    body = functools.partial(on_device, N, M) if (N, M) == (8, 4) else on_device_plain
    return jax.shard_map(
        body,
        mesh=mesh,
        in_specs=(P("dp", "mp"), P("dp", "mp"), P("dp", None)),
        out_specs=P("dp", "mp"),
        check_vma=False,
    )
```

```python
import functools

import jax
import jax.numpy as jnp
from jax import lax
from jax.experimental import pallas as pl
from jax.experimental.pallas import tpu as pltpu
from jax.sharding import PartitionSpec as P

radius = 0.005
epsilon = 1e-06
LAG = 1
MESH = pl.DeviceIdType.MESH


def on_device_plain(pre, weight, target):
    hidden = jax.nn.gelu(pre.astype(jnp.float32), approximate=False).astype(jnp.bfloat16)
    everyone = lax.all_gather(hidden, "dp", axis=0, tiled=True)
    entries = weight.shape[0] * weight.shape[1] * lax.axis_size("dp") * lax.axis_size("mp")

    def residual_of(matrix):
        partial_out = lax.dot_general(
            matrix, everyone, (((1,), (1,)), ((), ())), preferred_element_type=jnp.float32
        )
        summed = lax.psum(partial_out, "mp")
        return (summed - target.astype(jnp.float32)).astype(jnp.bfloat16)

    resid = residual_of(weight.astype(jnp.bfloat16))
    ascent = jnp.dot(resid, everyone, preferred_element_type=jnp.float32)
    ascent_ms = lax.psum(jnp.sum(ascent * ascent), ("dp", "mp")) / entries
    perturbed = (weight + radius * jnp.tanh(ascent / jnp.sqrt(ascent_ms + epsilon))).astype(
        jnp.bfloat16
    )
    resid_two = residual_of(perturbed)
    descent = jnp.dot(resid_two, everyone, preferred_element_type=jnp.float32)
    descent_ms = lax.psum(jnp.sum(descent * descent), ("dp", "mp")) / entries
    return descent / jnp.sqrt(descent_ms + epsilon)


def kernel(
    N, M, entries, C,
    hid_hbm, w_hbm, t_hbm, des_hbm, tot_ref,
    w, wl, h, a, tg, r1, own1, rcv1, pbuf, ssq, sm, sd, dsum,
    ld, ags, agr, cs, cr, ss, sr, od,
):
    rows, ff = w.shape
    tokens = tg.shape[1]
    blk = tokens // N
    half = rows // 2
    dp = lax.axis_index("dp")
    z = lax.axis_index("mp")
    b0 = lax.rem(dp, 2)
    b1 = lax.rem(dp // 2, 2)
    b2 = dp // 4
    ds_ = 1 - 2 * b0
    dx = 2 * (1 - 2 * b1)
    dy = 4 * (1 - 2 * b2)
    sib = dp + ds_
    p = dp + (1 - b0) * dx + b0 * dy
    q = dp + b0 * dx + (1 - b0) * dy
    diag = dp + dx + dy
    sibp = q + ds_
    sibq = p + ds_
    sibd = diag + ds_

    def load(i, src, dst):
        return pltpu.make_async_copy(src, dst, ld.at[i])

    def tok(b, lo=0, n=blk):
        return pl.ds(pl.multiple_of(b * blk + lo, 16), n)

    load_h = load(0, hid_hbm, h.at[tok(dp), :])
    load_w = load(1, w_hbm, w)
    load_t = load(2, t_hbm, tg)
    load_h.start()
    load_w.start()
    load_t.start()

    barrier = pltpu.get_barrier_semaphore()
    for k in range(1, N):
        pl.semaphore_signal(barrier, inc=1, device_id=(lax.rem(dp + k, N), z), device_id_type=MESH)
    for k in range(1, M):
        pl.semaphore_signal(barrier, inc=1, device_id=(dp, lax.rem(z + k, M)), device_id_type=MESH)
    pl.semaphore_wait(barrier, N + M - 2)

    def gather(i, block, to, lo=0, n=blk):
        return pltpu.make_async_remote_copy(
            src_ref=h.at[tok(block, lo, n), :], dst_ref=h.at[tok(block, lo, n), :],
            send_sem=ags.at[i], recv_sem=agr.at[i],
            device_id=(to, z), device_id_type=MESH,
        )

    hb = blk // 2
    S, PP, Q, SP, SQ, RPQ, RQP, SD = range(8)
    sends = {
        S: gather(S, dp, sib), PP: gather(PP, dp, p), Q: gather(Q, dp, q),
        SP: gather(SP, p, sib), SQ: gather(SQ, q, sib),
        RPQ: gather(RPQ, p, q, 0, hb), RQP: gather(RQP, q, p, hb, hb),
        SD: gather(SD, diag, sib),
    }
    recvs = {
        S: gather(S, sib, sib), PP: gather(PP, p, p), Q: gather(Q, q, q),
        SP: gather(SP, sibp, sib), SQ: gather(SQ, sibq, sib),
        RPQ: gather(RPQ, diag, q, 0, hb), RQP: gather(RQP, diag, p, hb, hb),
        SD: gather(SD, sibd, sib),
    }
    load_h.wait()
    sends[PP].start()
    sends[S].start()
    load_w.wait()

    def cast(i, _):
        rs = pl.ds(pl.multiple_of(i * 64, 64), 64)
        wl[rs, :] = w[rs, :].astype(jnp.bfloat16)
        return 0

    lax.fori_loop(0, rows // 64, cast, 0)
    load_t.wait()

    order = [dp, sib, p, sibp, q, sibq, diag, sibd]

    def block_of(c):
        out = order[0] * 0
        for k in range(N):
            out = out + order[k] * (1 - jnp.minimum(jnp.abs(c - k), 1))
        return out

    UP, DOWN, RUP, RDOWN = range(4)

    def move(kind, c, src, dst, to):
        return pltpu.make_async_remote_copy(
            src_ref=src, dst_ref=dst, send_sem=cs.at[kind, c], recv_sem=cr.at[kind, c],
            device_id=(dp, to), device_id_type=MESH,
        )

    zu = lax.rem(z + 1, M)
    zd = lax.rem(z + M - 1, M)

    def chain(produce, own_at, rcv_at, res_at, tgt_of, on_up, on_down, extra=None):
        def step(s, _):
            @pl.when(s < C)
            def _():
                produce(s)

            def reduce_one(kind, rkind, which, lag, is_head, is_tail, to, back):
                c = s - lag

                @pl.when((c >= 0) & (c < C))
                def _():
                    own = own_at(c, which)

                    @pl.when(jnp.logical_not(is_head))
                    def _():
                        move(kind, c, own, rcv_at(c, which), to).wait_recv()

                    @pl.when(jnp.logical_not(is_head | is_tail))
                    def _():
                        own[...] = own[...] + rcv_at(c, which)[...]

                    @pl.when(jnp.logical_not(is_tail))
                    def _():
                        move(kind, c, own, rcv_at(c, which), to).start()

                    @pl.when(is_tail)
                    def _():
                        total = own[...] + rcv_at(c, which)[...]
                        res_at(c, which)[...] = (
                            total - tgt_of(c, which)[...].astype(jnp.float32)
                        ).astype(jnp.bfloat16)
                        move(rkind, c, res_at(c, which), res_at(c, which), back).start()

            def back_one(rkind, which, lag, is_owner, is_last, to, done):
                c = s - lag

                @pl.when((c >= 0) & (c < C))
                def _():
                    @pl.when(jnp.logical_not(is_owner))
                    def _():
                        m = move(rkind, c, res_at(c, which), res_at(c, which), to)
                        m.wait_recv()

                        @pl.when(jnp.logical_not(is_last))
                        def _():
                            m.start()

                    if done is not None:
                        done(c)

            first, last = z == 0, z == M - 1
            reduce_one(UP, RUP, 0, LAG * z, first, last, zu, zd)
            reduce_one(DOWN, RDOWN, 1, LAG * (M - 1 - z), last, first, zd, zu)
            back_one(RUP, 0, LAG * (2 * (M - 1) - z), last, first, zd, on_up)
            back_one(RDOWN, 1, LAG * (M - 1 + z), first, last, zu, on_down)
            if extra is not None:
                extra(s)
            return 0

        lax.fori_loop(0, C + 2 * LAG * (M - 1), step, 0)

        def drain(c, _):
            @pl.when(z < M - 1)
            def _():
                move(UP, c, own_at(c, 0), rcv_at(c, 0), zu).wait_send()
                move(RDOWN, c, res_at(c, 1), res_at(c, 1), zu).wait_send()

            @pl.when(z > 0)
            def _():
                move(DOWN, c, own_at(c, 1), rcv_at(c, 1), zd).wait_send()
                move(RUP, c, res_at(c, 0), res_at(c, 0), zd).wait_send()

            return 0

        lax.fori_loop(0, C, drain, 0)

    def produce_one(s):
        @pl.when(s == 1)
        def _():
            recvs[S].wait_recv()

        @pl.when(s == 2)
        def _():
            recvs[PP].wait_recv()
            sends[SP].start()
            sends[Q].start()

        @pl.when(s == 3)
        def _():
            recvs[SP].wait_recv()

        @pl.when(s == 4)
        def _():
            recvs[Q].wait_recv()
            sends[RPQ].start()
            sends[RQP].start()
            sends[SQ].start()

        @pl.when(s == 5)
        def _():
            recvs[SQ].wait_recv()

        @pl.when(s == 6)
        def _():
            recvs[RPQ].wait_recv()
            recvs[RQP].wait_recv()
            sends[SD].start()

        @pl.when(s == 7)
        def _():
            recvs[SD].wait_recv()

        hb_ = h[tok(block_of(s)), :]
        own1[:, cols(s)] = lax.dot_general(
            wl[...], hb_, (((1,), (1,)), ((), ())), preferred_element_type=jnp.float32
        )

    def cols(c):
        return pl.ds(pl.multiple_of(block_of(c) * blk, blk), blk)

    def colwise(ref):
        return lambda c, which: ref.at[pl.ds(which * half, half), cols(c)]

    wide = ssq.shape[1]
    early = N // 2
    ready = early + 2 * LAG * (M - 1)
    tiles = ff // wide

    def ascent_of(lo, hi, cs_):
        left = jnp.concatenate([r1[:, cols(c)] for c in range(lo, hi)], axis=1)
        right = jnp.concatenate([h[tok(order[c]), cs_] for c in range(lo, hi)], axis=0)
        return jnp.dot(left, right, preferred_element_type=jnp.float32)

    def ascend_early(s):
        @pl.when((s >= ready) & (2 * (s - ready) < tiles))
        def _():
            for k in range(2):
                i = 2 * (s - ready) + k
                cs_ = pl.ds(pl.multiple_of(i * wide, wide), wide)
                a[:, cs_] = ascent_of(0, early, cs_)

    chain(
        produce_one, colwise(own1), colwise(rcv1), colwise(r1), colwise(tg), None, None,
        ascend_early,
    )
    for i in range(8):
        sends[i].wait_send()

    def total_squares(rnd):
        v = ssq[...]
        part = v[:, 0:128]
        for k in range(1, v.shape[1] // 128):
            part = part + v[:, 128 * k:128 * (k + 1)]

        def small(buf, lane, i, me, to):
            return pltpu.make_async_remote_copy(
                src_ref=buf.at[me], dst_ref=buf.at[me],
                send_sem=ss.at[rnd, lane, i], recv_sem=sr.at[rnd, lane, i],
                device_id=to, device_id_type=MESH,
            )

        mb = sm.at[rnd]
        db = sd.at[rnd]
        mb[z] = part
        up = [(dp, lax.rem(z + k, M)) for k in range(M)]
        dn = [lax.rem(z + M - k, M) for k in range(M)]
        for k in range(1, M):
            small(mb, 0, k, z, up[k]).start()
        for k in range(1, M):
            small(mb, 0, k, dn[k], up[k]).wait_recv()
        for k in range(1, M):
            small(mb, 0, k, z, up[k]).wait_send()
        got = mb[0]
        for k in range(1, M):
            got = got + mb[k]
        db[dp] = got
        upd = [(lax.rem(dp + k, N), z) for k in range(N)]
        dnd = [lax.rem(dp + N - k, N) for k in range(N)]
        for k in range(1, N):
            small(db, 1, k, dp, upd[k]).start()
        for k in range(1, N):
            small(db, 1, k, dnd[k], upd[k]).wait_recv()
        for k in range(1, N):
            small(db, 1, k, dp, upd[k]).wait_send()
        got = db[0]
        for k in range(1, N):
            got = got + db[k]
        return jnp.sum(jnp.sum(got, axis=0, keepdims=True), axis=1, keepdims=True)

    def squares(d):
        return (d * d).reshape(d.shape[0] // 8, 8, d.shape[1]).sum(axis=0)

    ssq[...] = jnp.zeros_like(ssq)

    def ascend(i, _):
        cs_ = pl.ds(pl.multiple_of(i * wide, wide), wide)
        d = a[:, cs_] + ascent_of(early, N, cs_)
        a[:, cs_] = d
        ssq[...] += squares(d)
        return 0

    lax.fori_loop(0, ff // wide, ascend, 0)
    scale = 1.0 / jnp.sqrt(total_squares(0) / entries + epsilon)
    ssq[...] = jnp.zeros_like(ssq)

    sub = half // C
    strip = tokens // 4

    def rws(c, which):
        return pl.ds(pl.multiple_of(which * half + c * sub, 16), sub)

    def produce_two(s):
        for which in range(2):
            rs = rws(s, which)
            pbuf[which * sub:(which + 1) * sub, :] = (
                w[rs, :] + radius * jnp.tanh(a[rs, :] * scale)
            ).astype(jnp.bfloat16)

        def part(i, _):
            ts = pl.ds(pl.multiple_of(i * strip, strip), strip)
            d = lax.dot_general(
                pbuf[...], h[ts, :], (((1,), (1,)), ((), ())), preferred_element_type=jnp.float32
            )
            own1[rws(s, 0), ts] = d[:sub]
            own1[rws(s, 1), ts] = d[sub:]
            return 0

        lax.fori_loop(0, tokens // strip, part, 0)

    def out_copy(c, which):
        return pltpu.make_async_copy(a.at[rws(c, which), :], des_hbm.at[rws(c, which), :], od.at[which, c])

    def descend(which):
        def run(c):
            def part(i, _):
                cs_ = pl.ds(pl.multiple_of(i * wide, wide), wide)
                d = jnp.dot(r1[rws(c, which), :], h[:, cs_], preferred_element_type=jnp.float32)
                a[rws(c, which), cs_] = d
                ssq[...] += squares(d)
                return 0

            lax.fori_loop(0, ff // wide, part, 0)
            out_copy(c, which).start()

        return run

    def rowwise(ref):
        return lambda c, which: ref.at[rws(c, which), :]

    chain(produce_two, rowwise(own1), rowwise(rcv1), rowwise(r1), rowwise(tg), descend(0), descend(1))
    tot_ref[...] = jnp.broadcast_to(total_squares(1), tot_ref.shape)

    def drain_out(c, _):
        out_copy(c, 0).wait()
        out_copy(c, 1).wait()
        return 0

    lax.fori_loop(0, C, drain_out, 0)


def on_device(N, M, pre, weight, target):
    hidden = jax.nn.gelu(pre.astype(jnp.float32), approximate=False).astype(jnp.bfloat16)
    rows, ff = weight.shape
    tokens = target.shape[1]
    entries = rows * ff * N * M
    C = N
    f32, bf16 = jnp.float32, jnp.bfloat16
    half = rows // 2
    any_ = pl.BlockSpec(memory_space=pl.ANY)
    descent, total = pl.pallas_call(
        functools.partial(kernel, N, M, float(entries), C),
        out_shape=(
            jax.ShapeDtypeStruct((rows, ff), f32),
            jax.ShapeDtypeStruct((8, 128), f32),
        ),
        in_specs=[any_, any_, any_],
        out_specs=(any_, pl.BlockSpec(memory_space=pltpu.VMEM)),
        scratch_shapes=[
            pltpu.VMEM((rows, ff), f32),
            pltpu.VMEM((rows, ff), bf16),
            pltpu.VMEM((tokens, ff), bf16),
            pltpu.VMEM((rows, ff), f32),
            pltpu.VMEM((rows, tokens), bf16),
            pltpu.VMEM((rows, tokens), bf16),
            pltpu.VMEM((rows, tokens), f32),
            pltpu.VMEM((rows, tokens), f32),
            pltpu.VMEM((2 * half // C, ff), bf16),
            pltpu.VMEM((8, 512), f32),
            pltpu.VMEM((2, M, 8, 128), f32),
            pltpu.VMEM((2, N, 8, 128), f32),
            pltpu.VMEM((8, 128), f32),
            pltpu.SemaphoreType.DMA((3,)),
            pltpu.SemaphoreType.DMA((8,)),
            pltpu.SemaphoreType.DMA((8,)),
            pltpu.SemaphoreType.DMA((4, C)),
            pltpu.SemaphoreType.DMA((4, C)),
            pltpu.SemaphoreType.DMA((2, 2, max(N, M))),
            pltpu.SemaphoreType.DMA((2, 2, max(N, M))),
            pltpu.SemaphoreType.DMA((2, C)),
        ],
        compiler_params=pltpu.CompilerParams(
            collective_id=0, has_side_effects=True, vmem_limit_bytes=41 << 20
        ),
    )(hidden, weight, target)
    return descent * (1.0 / jnp.sqrt(total[0, 0] / entries + epsilon))


def solution(mesh):
    N, M = mesh.shape["dp"], mesh.shape["mp"]
    body = functools.partial(on_device, N, M) if (N, M) == (8, 4) else on_device_plain
    return jax.shard_map(
        body,
        mesh=mesh,
        in_specs=(P("dp", "mp"), P("dp", "mp"), P("dp", None)),
        out_specs=P("dp", "mp"),
        check_vma=False,
    )
```
